256 devices in a mesh: env: 8 (over y, core), dof: 32 (over z, x).
Axes of the slice: x: 4, y: 4, z: 8, core: 2. Of those that a mesh axis runs over, the one named last changes fastest.
Arguments:
- system_matrix: bfloat16 [16, 8192, 8192], P('env', 'dof'), parts along dimension 0, as said below
- forces: float32 [8192, 16, 128], P('dof', 'env'), parts along dimension 1, may hold values from -6 to 6
Outputs:
- accelerations: float32 [8192, 16, 128], P('dof', 'env'), parts along dimension 1
- residual: float32 [8192, 16, 128], P('dof', 'env'), parts along dimension 1
The draws below stay inside these ranges and needn't reach their ends.
There are 8 independent parts, one for each index of `env`. The reference program is written for one: setup_inputs(seed, part) draws one part's arguments, and reference() takes and returns one part's arrays. A program takes and returns all parts, laid end to end along the dimension named above; each array names one. Nothing has to cross between parts.
Inputs may be any that keep to these rules, and one draw needn't show every extreme that they name: `system_matrix`: each environment's matrix is exactly symmetric and positive definite.
All inputs are finite; a program needn't handle non-finite values.
Results may differ from the reference program's by a relative error of at most 0.012.
Values may be sent and summed in bfloat16 or wider, within the bound.
No kernel may reach another device: no remote copies, remote signals or barrier semaphores. Data moves between devices by JAX's collectives and lax.ppermute only.
A program may use at most 64 MiB of HBM per device.

```python
import jax
import jax.numpy as jnp
from jax import lax

N = 8192
ENVS = 2
RHS = 128
ITERS = 4


def draw_system_matrix(key, part):
    key_noise = jax.random.fold_in(key, 21)
    key_scale = jax.random.fold_in(key, 22)
    key_shift = jax.random.fold_in(key, 23)
    scales = jnp.exp(jax.random.uniform(key_scale, (ENVS, N), jnp.float32, 0.0, 1.1513))
    shift = jax.random.uniform(key_shift, (ENVS, N), jnp.float32, 0.2, 0.5)

    def one_matrix(index):
        factor = jax.random.normal(jax.random.fold_in(key_noise, index), (N, N), jnp.float32)
        gram = jnp.dot(factor, factor.T, precision=lax.Precision.HIGHEST) * (1.0 / N)
        gram = 0.5 * (gram + gram.T)
        gram = gram + jnp.diag(shift[index])
        outer = scales[index][:, None] * scales[index][None, :]
        return (gram * outer).astype(jnp.bfloat16)
    return lax.map(one_matrix, jnp.arange(ENVS, dtype=jnp.int32))


def levels(stream_key, dims, cuts, least, high):
    level, own = 1.0, jax.random.fold_in(stream_key, 6)
    for dim, blocks in cuts:
        heights = jnp.exp(jax.random.uniform(jax.random.fold_in(own, dim), (blocks,), jnp.float32, least / len(cuts), high / len(cuts)))
        level = level * jnp.repeat(heights, dims[dim] // blocks).reshape([-1 if axis == dim else 1 for axis in range(len(dims))])
    return level


def gaussian(key, dims, scale, reach, pieces=(), kind=jnp.bfloat16):
    array = jax.random.normal(key, dims, jnp.float32) * scale
    if len(pieces) > 0:
        array = levels(key, dims, pieces, -0.22, 0.18) * array
    return jnp.clip(array, min=-reach, max=reach).astype(kind)


def setup_inputs(seed: int = 0, part: int = 0) -> dict:
    splits = jax.random.split(jax.random.key(seed), 3)
    own_keys = jax.random.split(jax.random.fold_in(splits[2], part), 3)
    return {
        "system_matrix": draw_system_matrix(jax.random.fold_in(jax.random.fold_in(splits[2], part), 71), part),
        "forces": gaussian(own_keys[1], (N, ENVS, RHS), 1.0, 6.0, ((0, 32),), jnp.float32),
    }


def apply_matrix(system_matrix, field):
    narrow = field.astype(jnp.bfloat16)
    columns = [jnp.dot(system_matrix[index], narrow[:, index, :], preferred_element_type=jnp.float32) for index in range(ENVS)]
    return jnp.stack(columns, axis=1)


def reference(system_matrix, forces):
    accelerations = jnp.zeros_like(forces)
    residual = forces
    direction = forces
    norm_now = jnp.sum(residual * residual, axis=0)
    for step in range(ITERS):
        image = apply_matrix(system_matrix, direction)
        alpha = norm_now / jnp.sum(direction * image, axis=0)
        accelerations = accelerations + alpha * direction
        residual = residual - alpha * image
        norm_next = jnp.sum(residual * residual, axis=0)
        direction = residual + (norm_next / norm_now) * direction
        norm_now = norm_next
    return accelerations, residual
```

```python
import functools

import jax
import jax.numpy as jnp
from jax import lax
from jax.experimental import pallas as pl
from jax.experimental.pallas import tpu as pltpu
from jax.sharding import Mesh
from jax.sharding import PartitionSpec as P

ITERS = 4
DOF = ("dof_0", "dof_1")
NZ, NX = 8, 4
ROWS, RHS = 256, 128
EXTRA = 16
X_STEPS = (0, 1, -1, 2)

X, R, D, W, S = (pl.ds(i * ROWS, ROWS) for i in range(5))
TAIL = 5 * ROWS


def thirds(value):
    parts = []
    for _ in range(3):
        part = value.astype(jnp.bfloat16)
        parts.append(part)
        value = value - part.astype(jnp.float32)
    return parts


def column_sum(value):
    return jnp.sum(value, axis=0, keepdims=True)


def multiply(where, env, rows, a_ref, pieces):
    z, x = where[0], where[1]
    total, extra = jnp.zeros((ROWS, RHS), jnp.float32), jnp.zeros((EXTRA, RHS), jnp.float32)
    for piece, step in zip(pieces, X_STEPS):
        for back in range(NZ):
            block = lax.rem(z + (NZ - back), NZ) * NX + lax.rem(x + (NX - step), NX)
            total += jnp.dot(
                a_ref[env, :, pl.ds(pl.multiple_of(block * ROWS, ROWS), ROWS)],
                piece[back, :ROWS, :],
                preferred_element_type=jnp.float32,
            )
            if rows > ROWS:
                extra += piece[back, ROWS:, :].astype(jnp.float32)
    return total, extra


def send(q, values, payload):
    rows = []
    for value in values:
        rows += thirds(value)
    rows.append(jnp.zeros((EXTRA - len(rows), RHS), jnp.bfloat16))
    payload[0, :ROWS, :] = q.astype(jnp.bfloat16)
    payload[0, ROWS:, :] = jnp.concatenate(rows, axis=0)


def first_kernel(env, where, a_ref, f_ref, *rest):
    pieces, (state, payload) = rest[:NX], rest[NX:]
    w, _ = multiply(where, env, ROWS, a_ref, pieces)
    f = f_ref[...]
    curve = column_sum(f * w)
    send(w, (column_sum(f * f), curve, curve, column_sum(w * w)), payload)
    state[X] = jnp.zeros_like(f)
    state[R] = f
    state[D] = f
    state[W] = w
    state[S] = w
    state[TAIL:, :] = jnp.zeros((8, RHS), jnp.float32)


def later_kernel(kind, env, where, a_ref, old, *rest):
    pieces, (new, *payload) = rest[:NX], rest[NX:]
    image, sums = multiply(where, env, ROWS + EXTRA, a_ref, pieces)
    norm, curve, cross, square = (column_sum(sums[3 * i : 3 * i + 3, :]) for i in range(4))
    alpha = norm / curve
    norm_next = norm - 2.0 * alpha * cross + alpha * alpha * square
    beta = norm_next / norm
    r, p, w, s = old[R], old[D], old[W], old[S]
    if kind == "second":
        change = alpha * image
    else:
        change = (alpha / old[TAIL : TAIL + 1, :]) * (s - image)
    s = s - change
    r = r - alpha * w
    new[X] = old[X] + alpha * p
    p = r + beta * p
    w = s + beta * w
    norm, curve = column_sum(r * r), column_sum(p * w)
    if kind == "last":
        tail = [norm, curve]
    else:
        send(r - alpha * w, (norm, curve, column_sum(r * w), column_sum(w * w)), payload[0])
        tail = [alpha, alpha]
    new[R] = r
    new[D] = p
    new[W] = w
    new[S] = s
    new[TAIL:, :] = jnp.concatenate([*tail, jnp.zeros((6, RHS), jnp.float32)], axis=0)


COST = pl.CostEstimate(flops=2 * ROWS * 8192 * RHS, bytes_accessed=8 << 20, transcendentals=0)
STATE = jax.ShapeDtypeStruct((TAIL + 8, RHS), jnp.float32)
PAYLOAD = jax.ShapeDtypeStruct((1, ROWS + EXTRA, RHS), jnp.bfloat16)


def call(kernel, outs, *inputs):
    in_vmem = pl.BlockSpec(memory_space=pltpu.VMEM)
    return pl.pallas_call(
        kernel,
        out_shape=outs,
        in_specs=[pl.BlockSpec(memory_space=pltpu.SMEM)] + [in_vmem] * (len(inputs) - 1),
        out_specs=[in_vmem] * len(outs),
        compiler_params=pltpu.CompilerParams(vmem_limit_bytes=24 << 20),
        cost_estimate=COST,
    )(*inputs)


def shifted(x, axis, by):
    size = lax.axis_size(axis)
    return lax.ppermute(x, axis, [(i, (i + by) % size) for i in range(size)])


def over_z(payload):
    return jnp.concatenate([payload] + [shifted(payload, "dof_0", by) for by in range(1, NZ)], axis=0)


def over_x(own):
    return [own] + [shifted(own, "dof_1", by) for by in X_STEPS[1:]]


def after(values, other):
    return lax.optimization_barrier((values, other))[0]


def taken_together(sums):
    copies = jnp.broadcast_to(sums.reshape(1, 1, -1), (NZ * NX, 1, sums.size))
    everything = lax.all_to_all(copies, DOF, split_axis=0, concat_axis=0, tiled=True)
    return jnp.sum(everything, axis=0).reshape(sums.shape)


def on_device(system_matrix, forces):
    where = jnp.stack([lax.axis_index("dof_0"), lax.axis_index("dof_1")]).astype(jnp.int32)
    where, forces = lax.optimization_barrier((where, forces))
    matrix = pltpu.with_memory_space_constraint(system_matrix, pltpu.VMEM)
    envs = range(2)
    state = [forces[:, env, :] for env in envs]
    own = [over_z(f.astype(jnp.bfloat16)[None]) for f in state]
    pieces = [over_x(own[0]), None]
    for step in range(ITERS):
        for env in envs:
            other = 1 - env
            if step < ITERS - 1 or env == 0:
                pieces[other] = over_x(own[other])
                pieces[env] = after(pieces[env], own[other])
            if step == 0:
                kernel, outs = first_kernel, [STATE, PAYLOAD]
            elif step < ITERS - 1:
                kernel, outs = functools.partial(later_kernel, "second" if step == 1 else "middle"), [STATE, PAYLOAD]
            else:
                kernel, outs = functools.partial(later_kernel, "last"), [STATE]
            got = call(functools.partial(kernel, env), outs, where, matrix, state[env], *pieces[env])
            state[env] = got[0]
            if step < ITERS - 1:
                own[env] = over_z(got[1])
    totals = taken_together(jnp.concatenate([s[TAIL : TAIL + 2] for s in state], axis=0))
    iterate, residual = [], []
    for env in envs:
        length = totals[2 * env] / totals[2 * env + 1]
        iterate.append(state[env][:ROWS] + length * state[env][2 * ROWS : 3 * ROWS])
        residual.append(state[env][ROWS : 2 * ROWS] - length * state[env][3 * ROWS : 4 * ROWS])
    return jnp.stack(iterate, axis=1), jnp.stack(residual, axis=1)


def solution(mesh):
    torus = Mesh(mesh.devices.reshape(mesh.shape["env"], NZ, NX), ("env", "dof_0", "dof_1"))
    placed = (P("env", DOF, None), P(DOF, "env", None))
    return jax.shard_map(
        on_device,
        mesh=torus,
        in_specs=placed,
        out_specs=(P(DOF, "env", None), P(DOF, "env", None)),
        check_vma=False,
    )
```

```python
import functools

import jax
import jax.numpy as jnp
from jax import lax
from jax.experimental import pallas as pl
from jax.experimental.pallas import tpu as pltpu
from jax.sharding import Mesh
from jax.sharding import PartitionSpec as P

ITERS = 4
DOF = ("dof_0", "dof_1")
NZ, NX = 8, 4
ROWS, RHS = 256, 128
EXTRA = 16
X_FROM = (0, NX - 1, 1, 2)
RING = [[(dz, dx) for dx in X_FROM] for dz in (0, 7, 6, 5, 1, 2, 3)]
RING += [[(4, dx) for dx in X_FROM[:2]], [(4, dx) for dx in X_FROM[2:]]]
ACROSS = [[(dz, dx) for dz in (0, 7, 6, 5, 4, 1, 2, 3)] for dx in X_FROM]
PLACES = (RING, RING)

X, R, D, W, S = (pl.ds(i * ROWS, ROWS) for i in range(5))
TAIL = 5 * ROWS


def thirds(value):
    parts = []
    for _ in range(3):
        part = value.astype(jnp.bfloat16)
        parts.append(part)
        value = value - part.astype(jnp.float32)
    return parts


def column_sum(value):
    return jnp.sum(value, axis=0, keepdims=True)


def multiply(where, env, rows, a_ref, pieces):
    z, x = where[0], where[1]
    total, extra = jnp.zeros((ROWS, RHS), jnp.float32), jnp.zeros((EXTRA, RHS), jnp.float32)
    for piece, places in zip(pieces, PLACES[env]):
        for i, (dz, dx) in enumerate(places):
            block = lax.rem(z + dz, NZ) * NX + lax.rem(x + dx, NX)
            total += jnp.dot(
                a_ref[env, :, pl.ds(pl.multiple_of(block * ROWS, ROWS), ROWS)],
                piece[i, :ROWS, :],
                preferred_element_type=jnp.float32,
            )
            if rows > ROWS:
                extra += piece[i, ROWS:, :].astype(jnp.float32)
    return total, extra


def send(q, values, payload):
    rows = []
    for value in values:
        rows += thirds(value)
    rows.append(jnp.zeros((EXTRA - len(rows), RHS), jnp.bfloat16))
    payload[0, :ROWS, :] = q.astype(jnp.bfloat16)
    payload[0, ROWS:, :] = jnp.concatenate(rows, axis=0)


def first_kernel(env, where, a_ref, f_ref, *rest):
    count = len(PLACES[env])
    pieces, (state, payload) = rest[:count], rest[count:]
    w, _ = multiply(where, env, ROWS, a_ref, pieces)
    f = f_ref[...]
    curve = column_sum(f * w)
    send(w, (column_sum(f * f), curve, curve, column_sum(w * w)), payload)
    state[X] = jnp.zeros_like(f)
    state[R] = f
    state[D] = f
    state[W] = w
    state[S] = w
    state[TAIL:, :] = jnp.zeros((8, RHS), jnp.float32)


def later_kernel(step, env, where, a_ref, old, *rest):
    count = len(PLACES[env])
    pieces, (*others, new, result) = rest[:count], rest[count:]
    image, sums = multiply(where, env, ROWS + EXTRA, a_ref, pieces)
    norm, curve, cross, square = (column_sum(sums[3 * i : 3 * i + 3, :]) for i in range(4))
    alpha = norm / curve
    norm_next = norm - 2.0 * alpha * cross + alpha * alpha * square
    beta = norm_next / norm
    r, p, w, s = old[R], old[D], old[W], old[S]
    if step == 1:
        change = alpha * image
    else:
        change = (alpha / old[TAIL : TAIL + 1, :]) * (s - image)
    s = s - change
    r = r - alpha * w
    new[X] = old[X] + alpha * p
    p = r + beta * p
    w = s + beta * w
    new[R] = r
    new[D] = p
    new[W] = w
    new[S] = s
    norm, curve = column_sum(r * r), column_sum(p * w)
    if step < ITERS - 1:
        send(r - alpha * w, (norm, curve, column_sum(r * w), column_sum(w * w)), result)
        tail = [alpha, alpha]
    else:
        tail = [norm, curve]
        if others:
            first = others[0]
            tail += [first[TAIL : TAIL + 1, :], first[TAIL + 1 : TAIL + 2, :]]
            for i, value in enumerate(tail):
                result[:, 0, i * RHS : (i + 1) * RHS] = jnp.broadcast_to(value, (NZ * NX, RHS))
        else:
            result[...] = jnp.zeros_like(result)
    tail.append(jnp.zeros((8 - len(tail), RHS), jnp.float32))
    new[TAIL:, :] = jnp.concatenate(tail, axis=0)


def final_kernel(sums, state0, state1, iterate, residual):
    totals = jnp.sum(sums[...], axis=0)
    for env, state in enumerate((state0, state1)):
        at = 2 * (1 - env) * RHS
        length = totals[:, at : at + RHS] / totals[:, at + RHS : at + 2 * RHS]
        iterate[:, env, :] = state[X] + length * state[D]
        residual[:, env, :] = state[R] - length * state[W]


def load_kernel(a_ref, out, sems):
    copies = []
    for i in range(LOADS):
        rows = pl.ds(i * ROWS // LOADS, ROWS // LOADS)
        copies.append(pltpu.make_async_copy(a_ref.at[:, rows], out.at[:, rows], sems.at[i]))
    for copy in copies:
        copy.start()
    for copy in copies:
        copy.wait()


LOADS = 8
COST = pl.CostEstimate(flops=2 * ROWS * 8192 * RHS, bytes_accessed=8 << 20, transcendentals=0)
STATE = jax.ShapeDtypeStruct((TAIL + 8, RHS), jnp.float32)
PAYLOAD = jax.ShapeDtypeStruct((1, ROWS + EXTRA, RHS), jnp.bfloat16)
SMALL = jax.ShapeDtypeStruct((8, RHS), jnp.float32)
SPREAD = jax.ShapeDtypeStruct((NZ * NX, 1, 4 * RHS), jnp.float32)
VMEM = pl.BlockSpec(memory_space=pltpu.VMEM)


def call(kernel, outs, *inputs):
    return pl.pallas_call(
        kernel,
        out_shape=outs,
        in_specs=[pl.BlockSpec(memory_space=pltpu.SMEM)] + [VMEM] * (len(inputs) - 1),
        out_specs=[VMEM] * len(outs),
        compiler_params=pltpu.CompilerParams(vmem_limit_bytes=24 << 20),
        cost_estimate=COST,
    )(*inputs)


def finish(sums, states):
    out = jax.ShapeDtypeStruct((ROWS, 2, RHS), jnp.float32)
    return pl.pallas_call(
        final_kernel,
        out_shape=[out, out],
        in_specs=[VMEM] * 3,
        out_specs=[VMEM] * 2,
        compiler_params=pltpu.CompilerParams(vmem_limit_bytes=16 << 20),
    )(sums, *states)


def load(matrix):
    return pl.pallas_call(
        load_kernel,
        out_shape=jax.ShapeDtypeStruct(matrix.shape, matrix.dtype),
        in_specs=[pl.BlockSpec(memory_space=pltpu.HBM)],
        out_specs=VMEM,
        scratch_shapes=[pltpu.SemaphoreType.DMA((LOADS,))],
        compiler_params=pltpu.CompilerParams(vmem_limit_bytes=16 << 20),
        cost_estimate=pl.CostEstimate(flops=0, bytes_accessed=2 * matrix.size * 2, transcendentals=0),
    )(matrix)


def shifted(x, axis, by):
    size = lax.axis_size(axis)
    return lax.ppermute(x, axis, [(i, (i + by) % size) for i in range(size)])


def over_x(block):
    return [block] + [shifted(block, "dof_1", by) for by in (1, -1, 2)]


def ring(payload):
    block = jnp.concatenate(over_x(payload), axis=0)
    up, down = [block], [block]
    for _ in range(NZ // 2 - 1):
        up.append(shifted(up[-1], "dof_0", 1))
        down.append(shifted(down[-1], "dof_0", -1))
    ends = [shifted(up[-1][: NX // 2], "dof_0", 1), shifted(down[-1][NX // 2 :], "dof_0", -1)]
    return up + down[1:] + ends


def across(payload):
    up, down = [payload], [payload]
    for _ in range(NZ // 2 - 1):
        up.append(shifted(up[-1], "dof_0", 1))
        down.append(shifted(down[-1], "dof_0", -1))
    up.append(shifted(up[-1], "dof_0", 1))
    return over_x(jnp.concatenate(up + down[1:], axis=0))


def on_device(system_matrix, forces):
    where = jnp.stack([lax.axis_index("dof_0"), lax.axis_index("dof_1")]).astype(jnp.int32)
    where, forces = lax.optimization_barrier((where, forces))
    matrix = load(system_matrix)
    state = [forces[:, env, :] for env in range(2)]
    payload = [f.astype(jnp.bfloat16)[None] for f in state]
    for step in range(ITERS):
        for env, gather in enumerate((ring, ring)):
            kernel = functools.partial(later_kernel, step) if step else first_kernel
            inputs = [where, matrix, state[env], *gather(payload[env])]
            out = PAYLOAD
            if step == ITERS - 1:
                out = (SMALL, SPREAD)[env]
                inputs += state[:env]
            state[env], payload[env] = call(functools.partial(kernel, env), [STATE, out], *inputs)
    sums = lax.all_to_all(payload[1], DOF, split_axis=0, concat_axis=0, tiled=True)
    return tuple(finish(sums, state))


def solution(mesh):
    torus = Mesh(mesh.devices.reshape(mesh.shape["env"], NZ, NX), ("env", "dof_0", "dof_1"))
    placed = (P("env", DOF, None), P(DOF, "env", None))
    return jax.shard_map(
        on_device,
        mesh=torus,
        in_specs=placed,
        out_specs=(P(DOF, "env", None), P(DOF, "env", None)),
        check_vma=False,
    )
```

```python
import functools

import jax
import jax.numpy as jnp
from jax import lax
from jax.experimental import pallas as pl
from jax.experimental.pallas import tpu as pltpu
from jax.sharding import Mesh
from jax.sharding import PartitionSpec as P

ITERS = 4
DOF = ("dof_0", "dof_1")
NZ, NX = 8, 4
ROWS, RHS = 256, 128
EXTRA = 16
X_FROM = (0, NX - 1, 1, 2)
RING = [[(dz, dx) for dx in X_FROM] for dz in (0, 7, 6, 5, 1, 2, 3)]
RING += [[(4, dx) for dx in X_FROM[:2]], [(4, dx) for dx in X_FROM[2:]]]
EARLY, LATE = (0, 1, 2, 4, 5), (3, 6, 7, 8)

X, R, D, W, S = (pl.ds(i * ROWS, ROWS) for i in range(5))
TAIL = 5 * ROWS


def thirds(value):
    parts = []
    for _ in range(3):
        part = value.astype(jnp.bfloat16)
        parts.append(part)
        value = value - part.astype(jnp.float32)
    return parts


def column_sum(value):
    return jnp.sum(value, axis=0, keepdims=True)


def multiply(where, env, rows, a_ref, pieces, which, total, extra):
    z, x = where[0], where[1]
    for piece, places in zip(pieces, [RING[i] for i in which]):
        for i, (dz, dx) in enumerate(places):
            block = lax.rem(z + dz, NZ) * NX + lax.rem(x + dx, NX)
            total += jnp.dot(
                a_ref[env, :, pl.ds(pl.multiple_of(block * ROWS, ROWS), ROWS)],
                piece[i, :ROWS, :],
                preferred_element_type=jnp.float32,
            )
            if rows > ROWS:
                extra += piece[i, ROWS:, :].astype(jnp.float32)
    return total, extra


def send(q, values, payload):
    rows = []
    for value in values:
        rows += thirds(value)
    rows.append(jnp.zeros((EXTRA - len(rows), RHS), jnp.bfloat16))
    payload[0, :ROWS, :] = q.astype(jnp.bfloat16)
    payload[0, ROWS:, :] = jnp.concatenate(rows, axis=0)


def early_kernel(rows, env, where, a_ref, *rest):
    pieces, (out,) = rest[: len(EARLY)], rest[len(EARLY) :]
    zeros = jnp.zeros((ROWS, RHS), jnp.float32), jnp.zeros((EXTRA, RHS), jnp.float32)
    out[:ROWS, :], out[ROWS:, :] = multiply(where, env, rows, a_ref, pieces, EARLY, *zeros)


def first_kernel(env, where, a_ref, f_ref, early, *rest):
    count = len(LATE)
    pieces, (state, payload) = rest[:count], rest[count:]
    w, _ = multiply(where, env, ROWS, a_ref, pieces, LATE, early[:ROWS, :], None)
    f = f_ref[...]
    curve = column_sum(f * w)
    send(w, (column_sum(f * f), curve, curve, column_sum(w * w)), payload)
    state[X] = jnp.zeros_like(f)
    state[R] = f
    state[D] = f
    state[W] = w
    state[S] = w
    state[TAIL:, :] = jnp.zeros((8, RHS), jnp.float32)


def later_kernel(step, env, where, a_ref, old, early, *rest):
    count = len(LATE)
    pieces, (*others, new, result) = rest[:count], rest[count:]
    image, sums = multiply(where, env, ROWS + EXTRA, a_ref, pieces, LATE, early[:ROWS, :], early[ROWS:, :])
    norm, curve, cross, square = (column_sum(sums[3 * i : 3 * i + 3, :]) for i in range(4))
    alpha = norm / curve
    norm_next = norm - 2.0 * alpha * cross + alpha * alpha * square
    beta = norm_next / norm
    r, p, w, s = old[R], old[D], old[W], old[S]
    if step == 1:
        change = alpha * image
    else:
        change = (alpha / old[TAIL : TAIL + 1, :]) * (s - image)
    s = s - change
    r = r - alpha * w
    new[X] = old[X] + alpha * p
    p = r + beta * p
    w = s + beta * w
    new[R] = r
    new[D] = p
    new[W] = w
    new[S] = s
    norm, curve = column_sum(r * r), column_sum(p * w)
    if step < ITERS - 1:
        send(r - alpha * w, (norm, curve, column_sum(r * w), column_sum(w * w)), result)
        tail = [alpha, alpha]
    else:
        tail = [norm, curve]
        if others:
            first = others[0]
            tail += [first[TAIL : TAIL + 1, :], first[TAIL + 1 : TAIL + 2, :]]
            for i, value in enumerate(tail):
                result[:, 0, i * RHS : (i + 1) * RHS] = jnp.broadcast_to(value, (NZ * NX, RHS))
        else:
            result[...] = jnp.zeros_like(result)
    tail.append(jnp.zeros((8 - len(tail), RHS), jnp.float32))
    new[TAIL:, :] = jnp.concatenate(tail, axis=0)


def final_kernel(sums, state0, state1, iterate, residual):
    totals = jnp.sum(sums[...], axis=0)
    for env, state in enumerate((state0, state1)):
        at = 2 * (1 - env) * RHS
        length = totals[:, at : at + RHS] / totals[:, at + RHS : at + 2 * RHS]
        iterate[:, env, :] = state[X] + length * state[D]
        residual[:, env, :] = state[R] - length * state[W]


def load_kernel(a_ref, out, sems):
    copies = []
    for i in range(LOADS):
        rows = pl.ds(i * ROWS // LOADS, ROWS // LOADS)
        copies.append(pltpu.make_async_copy(a_ref.at[:, rows], out.at[:, rows], sems.at[i]))
    for copy in copies:
        copy.start()
    for copy in copies:
        copy.wait()


LOADS = 8
COST = pl.CostEstimate(flops=ROWS * 8192 * RHS, bytes_accessed=4 << 20, transcendentals=0)
STATE = jax.ShapeDtypeStruct((TAIL + 8, RHS), jnp.float32)
PAYLOAD = jax.ShapeDtypeStruct((1, ROWS + EXTRA, RHS), jnp.bfloat16)
PARTIAL = jax.ShapeDtypeStruct((ROWS + EXTRA, RHS), jnp.float32)
SMALL = jax.ShapeDtypeStruct((8, RHS), jnp.float32)
SPREAD = jax.ShapeDtypeStruct((NZ * NX, 1, 4 * RHS), jnp.float32)
VMEM = pl.BlockSpec(memory_space=pltpu.VMEM)


def call(kernel, outs, *inputs):
    return pl.pallas_call(
        kernel,
        out_shape=outs,
        in_specs=[pl.BlockSpec(memory_space=pltpu.SMEM)] + [VMEM] * (len(inputs) - 1),
        out_specs=[VMEM] * len(outs),
        compiler_params=pltpu.CompilerParams(vmem_limit_bytes=24 << 20),
        cost_estimate=COST,
    )(*inputs)


def finish(sums, states):
    out = jax.ShapeDtypeStruct((ROWS, 2, RHS), jnp.float32)
    return pl.pallas_call(
        final_kernel,
        out_shape=[out, out],
        in_specs=[VMEM] * 3,
        out_specs=[VMEM] * 2,
        compiler_params=pltpu.CompilerParams(vmem_limit_bytes=16 << 20),
    )(sums, *states)


def load(matrix):
    return pl.pallas_call(
        load_kernel,
        out_shape=jax.ShapeDtypeStruct(matrix.shape, matrix.dtype),
        in_specs=[pl.BlockSpec(memory_space=pltpu.HBM)],
        out_specs=VMEM,
        scratch_shapes=[pltpu.SemaphoreType.DMA((LOADS,))],
        compiler_params=pltpu.CompilerParams(vmem_limit_bytes=16 << 20),
        cost_estimate=pl.CostEstimate(flops=0, bytes_accessed=2 * matrix.size * 2, transcendentals=0),
    )(matrix)


def shifted(x, axis, by):
    size = lax.axis_size(axis)
    return lax.ppermute(x, axis, [(i, (i + by) % size) for i in range(size)])


def over_x(block):
    return [block] + [shifted(block, "dof_1", by) for by in (1, -1, 2)]


def ring(block):
    up, down = [block], [block]
    for _ in range(NZ // 2 - 1):
        down.append(shifted(down[-1], "dof_0", -1))
        up.append(shifted(up[-1], "dof_0", 1))
    ends = [shifted(up[-1][: NX // 2], "dof_0", 1), shifted(down[-1][NX // 2 :], "dof_0", -1)]
    return up + down[1:] + ends


RINGS = (ring, ring)


def on_device(system_matrix, forces):
    where = jnp.stack([lax.axis_index("dof_0"), lax.axis_index("dof_1")]).astype(jnp.int32)
    where, forces = lax.optimization_barrier((where, forces))
    matrix = load(system_matrix)
    state = [forces[:, env, :] for env in range(2)]
    payload = [f.astype(jnp.bfloat16)[None] for f in state]
    for step in range(ITERS):
        for env, gather in enumerate(RINGS):
            kernel = functools.partial(later_kernel, step) if step else first_kernel
            block = jnp.concatenate(over_x(payload[env]), axis=0)
            if step == 0 and env == 0:
                block, matrix = lax.optimization_barrier((block, matrix))
            pieces = gather(block)
            rows = ROWS + EXTRA if step else ROWS
            (early,) = call(
                functools.partial(early_kernel, rows, env), [PARTIAL], where, matrix, *[pieces[i] for i in EARLY]
            )
            inputs = [where, matrix, state[env], early, *[pieces[i] for i in LATE]]
            out = PAYLOAD
            if step == ITERS - 1:
                out = (SMALL, SPREAD)[env]
                inputs += state[:env]
            state[env], payload[env] = call(functools.partial(kernel, env), [STATE, out], *inputs)
    sums = lax.all_to_all(payload[1], DOF, split_axis=0, concat_axis=0, tiled=True)
    return tuple(finish(sums, state))


def solution(mesh):
    torus = Mesh(mesh.devices.reshape(mesh.shape["env"], NZ, NX), ("env", "dof_0", "dof_1"))
    placed = (P("env", DOF, None), P(DOF, "env", None))
    return jax.shard_map(
        on_device,
        mesh=torus,
        in_specs=placed,
        out_specs=(P(DOF, "env", None), P(DOF, "env", None)),
        check_vma=False,
    )
```
